32 devices in a mesh: rows: 8 (over z, y), rhs: 4 (over x, core).
Axes of the slice: x: 2, y: 2, z: 4, core: 2. Of those that a mesh axis runs over, the one named last changes fastest.
Arguments:
- rhs: float32 [8192, 2048], P('rows', 'rhs'), parts along dimension 1, may hold values from -6 to 6
- leaf_inverse: float32 [8192, 1024], P('rows'), may hold values from -0.1875 to 0.1875
- basis_left: float32 [3, 8192, 128], P(None, 'rows'), may hold values from -0.5 to 0.5
- basis_right: float32 [3, 8192, 128], P(None, 'rows'), may hold values from -0.09375 to 0.09375
- cores: float32 [7, 256, 256], replicated, may hold values from -0.375 to 0.375
Outputs:
- solution: float32 [8192, 2048], P('rows', 'rhs'), parts along dimension 1
The draws below stay inside these ranges and needn't reach their ends.
There are 4 independent parts, one for each index of `rhs`. The reference program is written for one: setup_inputs(seed, part) draws one part's arguments, and reference() takes and returns one part's arrays. A program takes and returns all parts, laid end to end along the dimension named above; an argument that names none is the same for every part. Nothing has to cross between parts.
All inputs are finite; a program needn't handle non-finite values.
Results may differ from the reference program's by a relative error of at most 0.00011.
Values sent between devices are 32-bit elements; how exact they have to be, the bound alone decides.
A program may use at most 64 MiB of HBM per device.

```python
import jax
import jax.numpy as jnp
from jax import lax

LEAF = 1024
R = 128
COLS = 512
LEVELS = 3
N = 8192
N_ROWS = 8


def shard_levels(stream_key, dims, shards, smallest, high):
    level, own = 1.0, jax.random.fold_in(stream_key, 6)
    for dim, parts in shards:
        heights = jnp.exp(jax.random.uniform(jax.random.fold_in(own, dim), (parts,), jnp.float32, smallest / len(shards), high / len(shards)))
        level = level * jnp.repeat(heights, dims[dim] // parts).reshape([-1 if axis == dim else 1 for axis in range(len(dims))])
    return level


def normal_values(own_key, dims, spread, most, split=(), held_as=jnp.bfloat16):
    array = spread * jax.random.normal(own_key, dims, jnp.float32)
    if split:
        array = array * shard_levels(own_key, dims, split, -0.22, 0.18)
    return jnp.clip(array, -most, most).astype(held_as)


def setup_inputs(seed: int = 0, part: int = 0) -> dict:
    seeds = jax.random.split(jax.random.key(seed), 6)
    part_keys = jax.random.split(jax.random.fold_in(seeds[5], part), 6)
    rhs = normal_values(part_keys[0], (N, COLS), 1.0, 6.0, ((0, 8),), jnp.float32)
    leaf_inverse = normal_values(seeds[1], (N, LEAF), LEAF ** -0.5, 0.1875, ((0, 8),), jnp.float32)
    basis_left = normal_values(seeds[2], (LEVELS, N, R), R ** -0.5, 0.5, ((1, 8),), jnp.float32)
    basis_right = normal_values(seeds[3], (LEVELS, N, R), (N // 2) ** -0.5, 0.09375, ((1, 8),), jnp.float32)
    cores = normal_values(seeds[4], (2 ** LEVELS - 1, 2 * R, 2 * R), (2 * R) ** -0.5, 0.375, (), jnp.float32)
    return {"rhs": rhs, "leaf_inverse": leaf_inverse, "basis_left": basis_left, "basis_right": basis_right, "cores": cores}


def reference(rhs, leaf_inverse, basis_left, basis_right, cores):
    highest = lax.Precision.HIGHEST
    total_rows = rhs.shape[0]
    columns = rhs.shape[1]
    leaves = leaf_inverse.reshape(N_ROWS, LEAF, LEAF)
    current = jnp.einsum('lij,ljc->lic', leaves, rhs.reshape(N_ROWS, LEAF, columns), precision=highest)
    current = current.reshape(total_rows, columns)
    for level_index in range(LEVELS, 0, -1):
        blocks = 2 ** level_index
        height = total_rows // blocks
        right_basis = basis_right[level_index - 1].reshape(blocks, height, R)
        left_basis = basis_left[level_index - 1].reshape(blocks, height, R)
        shaped = current.reshape(blocks, height, columns)
        partial_value = jnp.einsum('bnr,bnc->brc', right_basis, shaped, precision=highest)
        stacked = partial_value.reshape(blocks // 2, 2 * R, columns)
        core_block = cores[blocks // 2 - 1: blocks - 1]
        coefficients = jnp.einsum('jst,jtc->jsc', core_block, stacked, precision=highest).reshape(blocks, R, columns)
        shaped = shaped - jnp.einsum('bnr,brc->bnc', left_basis, coefficients, precision=highest)
        current = shaped.reshape(total_rows, columns)
    return current
```

```python
import functools

import jax
import jax.numpy as jnp
from jax import lax
from jax.experimental import pallas as pl
from jax.experimental.pallas import tpu as pltpu
from jax.sharding import PartitionSpec as P

F32 = jnp.float32
BF16 = jnp.bfloat16


def swapped(x, axis, apart):
    return lax.ppermute(x, axis, [(i, i ^ 1 << apart) for i in range(lax.axis_size(axis))])


def general(rhs, leaf_inverse, basis_left, basis_right, cores):
    highest = lax.Precision.HIGHEST
    current = jnp.dot(leaf_inverse, rhs, precision=highest, preferred_element_type=F32)
    devices = lax.axis_size("rows")
    tree_depth = devices.bit_length() - 1
    position = lax.axis_index("rows")
    rank_size = basis_left.shape[2]
    for level_index in range(basis_left.shape[0], 0, -1):
        span_devices = devices >> level_index
        child_index = position // span_devices
        node_index = child_index // 2
        half_index = child_index % 2
        child_total = lax.dot_general(
            basis_right[level_index - 1],
            current,
            (((0,), (0,)), ((), ())),
            precision=highest,
            preferred_element_type=F32,
        )
        for bit_number in range(tree_depth - level_index):
            child_total = child_total + swapped(child_total, "rows", bit_number)
        sibling = swapped(child_total, "rows", tree_depth - level_index)
        stacked = jnp.where(
            half_index == 0,
            jnp.concatenate([child_total, sibling], axis=0),
            jnp.concatenate([sibling, child_total], axis=0),
        )
        core_block = lax.dynamic_index_in_dim(
            cores, 2 ** (level_index - 1) - 1 + node_index, 0, keepdims=False
        )
        core_rows = lax.dynamic_slice_in_dim(core_block, half_index * rank_size, rank_size, 0)
        coefficients = jnp.dot(core_rows, stacked, precision=highest, preferred_element_type=F32)
        current = current - jnp.dot(
            basis_left[level_index - 1], coefficients, precision=highest, preferred_element_type=F32
        )
    return current


def split(x):
    high = x.astype(BF16)
    return high, (x - high.astype(F32)).astype(BF16)


def weights(x):
    high, low = split(x)
    return jnp.concatenate([high, high, low], axis=1)


def values(x):
    high, low = split(x)
    return jnp.concatenate([high, low, high], axis=0)


def dot(a, b):
    return jnp.dot(a, b, preferred_element_type=F32)


def kernel(
    rhs_h, leaf_h, left_h, right_h, cores_h, out_h,
    rhs, leaf, left, right, core,
    leaf3, right3, left3, core3, mix3, x3, y3,
    y, proj, mix, up, upmix, top, c3s, c2s,
    in_sem, out_sem, send_y, recv_y, send_z, recv_z, send_t, recv_t,
):
    n, cols = rhs.shape
    rank = left.shape[2]
    chunks, _, _, wide = proj.shape
    me = lax.axis_index("rows")
    bit_y = lax.rem(me, 2)
    bit_z = lax.rem(me // 2, 2)
    bit_t = me // 4
    at_y = me + 1 - 2 * bit_y
    at_z = me + 2 - 4 * bit_z
    at_t = me + 4 - 8 * bit_t

    blocks = 4
    tall = n // blocks
    loads = []

    def load(src, dst):
        copy = pltpu.make_async_copy(src, dst, in_sem.at[len(loads)])
        copy.start()
        loads.append(copy)
        return copy

    load_right = load(right_h, right)
    load_left = load(left_h, left)
    load_rhs = load(rhs_h, rhs)
    load_leaf = [
        load(leaf_h.at[pl.ds(i * tall, tall), :], leaf.at[pl.ds(i * tall, tall), :])
        for i in range(blocks)
    ]
    load_core = [
        load(cores_h.at[3 + me // 2], core.at[2]),
        load(cores_h.at[1 + me // 4], core.at[1]),
        load(cores_h.at[0], core.at[0]),
    ]

    barrier = pltpu.get_barrier_semaphore()
    for other in (at_y, at_z, at_t):
        pl.semaphore_signal(
            barrier, inc=1, device_id={"rows": other}, device_id_type=pl.DeviceIdType.MESH
        )

    sends = []

    def send(ref, slot, other, send_sem, recv_sem, k):
        copy = pltpu.make_async_remote_copy(
            src_ref=ref.at[slot],
            dst_ref=ref.at[slot],
            send_sem=send_sem.at[k],
            recv_sem=recv_sem.at[k],
            device_id={"rows": other},
            device_id_type=pl.DeviceIdType.MESH,
        )
        copy.start()
        sends.append(copy)
        return copy

    load_right.wait()
    for i in range(3):
        right3[pl.ds(i * rank, rank), :] = weights(jnp.transpose(right[2 - i]))
    load_left.wait()
    for i in range(3):
        left3[:, pl.ds(i * 3 * rank, 3 * rank)] = weights(left[2 - i])
    mix[bit_y, pl.ds(0, 2 * rank), :] = dot(right3[pl.ds(rank, 2 * rank), :], values(left[2]))
    mix[bit_y, pl.ds(2 * rank, rank), :] = dot(right3[pl.ds(2 * rank, rank), :], values(left[1]))

    pl.semaphore_wait(barrier, 3)
    mix_y = send(mix, bit_y, at_y, send_y, recv_y, chunks)

    load_rhs.wait()
    for i in range(blocks):
        load_leaf[i].wait()
        leaf3[pl.ds(i * tall, tall), :] = weights(leaf[pl.ds(i * tall, tall), :])
    got_y = [None] * chunks
    half = 2 * wide
    for h in range(cols // half):
        x3[...] = values(rhs[:, pl.ds(h * half, half)])
        product = dot(leaf3[...], x3[...])
        y3[...] = values(product)
        for j in range(2):
            y[2 * h + j] = product[:, j * wide:(j + 1) * wide]
        partial = dot(right3[...], y3[...])
        for j in range(2):
            c = 2 * h + j
            proj[c, bit_y] = partial[:, j * wide:(j + 1) * wide]
            got_y[c] = send(proj.at[c], bit_y, at_y, send_y, recv_y, c)

    for copy in load_core:
        copy.wait()
    for i in range(3):
        core3[i] = weights(core[i])
    mix_y.wait_recv()
    upmix[bit_z] = mix[0, pl.ds(2 * rank, rank), :] + mix[1, pl.ds(2 * rank, rank), :]
    mix_z = send(upmix, bit_z, at_z, send_z, recv_z, chunks)
    mix3[...] = weights(
        jnp.concatenate([mix[0, pl.ds(0, 2 * rank), :], mix[1, pl.ds(0, 2 * rank), :]], axis=1)
    )
    got_z = [None] * chunks
    got_t = [None] * chunks
    upmix3 = []
    outs = []

    def first(c):
        got_y[c].wait_recv()
        stack = jnp.concatenate([proj[c, 0, pl.ds(0, rank), :], proj[c, 1, pl.ds(0, rank), :]], axis=0)
        coeff = dot(core3[2], values(stack))
        rest = proj[c, 0, pl.ds(rank, 2 * rank), :] + proj[c, 1, pl.ds(rank, 2 * rank), :]
        up[c, bit_z] = rest - dot(mix3[...], values(coeff))
        got_z[c] = send(up.at[c], bit_z, at_z, send_z, recv_z, c)
        c3s[0] = coeff[:rank]
        c3s[1] = coeff[rank:]
        y[c] = y[c] - dot(left3[:, pl.ds(0, 3 * rank)], values(c3s[bit_y]))

    def second(c):
        if not upmix3:
            mix_z.wait_recv()
            upmix3.append(weights(jnp.concatenate([upmix[0], upmix[1]], axis=1)))
        got_z[c].wait_recv()
        stack = jnp.concatenate([up[c, 0, pl.ds(0, rank), :], up[c, 1, pl.ds(0, rank), :]], axis=0)
        coeff = dot(core3[1], values(stack))
        rest = up[c, 0, pl.ds(rank, rank), :] + up[c, 1, pl.ds(rank, rank), :]
        top[c, bit_t] = rest - dot(upmix3[0], values(coeff))
        got_t[c] = send(top.at[c], bit_t, at_t, send_t, recv_t, c)
        c2s[0] = coeff[:rank]
        c2s[1] = coeff[rank:]
        y[c] = y[c] - dot(left3[:, pl.ds(3 * rank, 3 * rank)], values(c2s[bit_z]))

    def third(c):
        got_t[c].wait_recv()
        stack = jnp.concatenate([top[c, 0], top[c, 1]], axis=0)
        coeff = dot(core3[0, pl.ds(bit_t * rank, rank), :], values(stack))
        y[c] = y[c] - dot(left3[:, pl.ds(6 * rank, 3 * rank)], values(coeff))
        copy = pltpu.make_async_copy(y.at[c], out_h.at[:, pl.ds(c * wide, wide)], out_sem.at[c])
        copy.start()
        outs.append(copy)

    for step in range(chunks + 3):
        if 0 <= step < chunks:
            first(step)
        if 0 <= step - 1 < chunks:
            second(step - 1)
        if 0 <= step - 2 < chunks:
            third(step - 2)

    for copy in sends:
        copy.wait_send()
    for copy in outs:
        copy.wait()


def on_device(rhs, leaf_inverse, basis_left, basis_right, cores):
    levels, n, rank = basis_left.shape
    cols = rhs.shape[1]
    if levels != 3 or lax.axis_size("rows") != 8 or cols % 256 or n % 1024 or rank % 128:
        return general(rhs, leaf_inverse, basis_left, basis_right, cores)
    wide = 128
    chunks = cols // wide
    any_space = pl.BlockSpec(memory_space=pl.ANY)
    dma = pltpu.SemaphoreType.DMA
    vmem = pltpu.VMEM
    return pl.pallas_call(
        kernel,
        out_shape=jax.ShapeDtypeStruct((n, cols), F32),
        in_specs=[any_space] * 5,
        out_specs=any_space,
        scratch_shapes=[
            vmem((n, cols), F32),
            vmem(leaf_inverse.shape, F32),
            vmem((3, n, rank), F32),
            vmem((3, n, rank), F32),
            vmem((3, 2 * rank, 2 * rank), F32),
            vmem((n, 3 * n), BF16),
            vmem((3 * rank, 3 * n), BF16),
            vmem((n, 9 * rank), BF16),
            vmem((3, 2 * rank, 6 * rank), BF16),
            vmem((2 * rank, 6 * rank), BF16),
            vmem((3 * n, 2 * wide), BF16),
            vmem((3 * n, 2 * wide), BF16),
            vmem((chunks, n, wide), F32),
            vmem((chunks, 2, 3 * rank, wide), F32),
            vmem((2, 3 * rank, rank), F32),
            vmem((chunks, 2, 2 * rank, wide), F32),
            vmem((2, rank, rank), F32),
            vmem((chunks, 2, rank, wide), F32),
            vmem((2, rank, wide), F32),
            vmem((2, rank, wide), F32),
            dma((10,)),
            dma((chunks,)),
            dma((chunks + 1,)),
            dma((chunks + 1,)),
            dma((chunks + 1,)),
            dma((chunks + 1,)),
            dma((chunks,)),
            dma((chunks,)),
        ],
        compiler_params=pltpu.CompilerParams(
            collective_id=0, has_side_effects=True, vmem_limit_bytes=56 * 1024 * 1024
        ),
        name="tree",
    )(rhs, leaf_inverse, basis_left, basis_right, cores)


def solution(mesh):
    placed = (P("rows", "rhs"), P("rows", None), P(None, "rows", None), P(None, "rows", None), P())
    return jax.shard_map(
        on_device, mesh=mesh, in_specs=placed, out_specs=P("rows", "rhs"), check_vma=False
    )
```

```python
import jax
import jax.numpy as jnp
from jax import lax
from jax.experimental import pallas as pl
from jax.experimental.pallas import tpu as pltpu
from jax.sharding import PartitionSpec as P

F32 = jnp.float32
BF16 = jnp.bfloat16


def swapped(x, axis, apart):
    return lax.ppermute(x, axis, [(i, i ^ 1 << apart) for i in range(lax.axis_size(axis))])


def general(rhs, leaf_inverse, basis_left, basis_right, cores):
    highest = lax.Precision.HIGHEST
    current = jnp.dot(leaf_inverse, rhs, precision=highest, preferred_element_type=F32)
    devices = lax.axis_size("rows")
    tree_depth = devices.bit_length() - 1
    position = lax.axis_index("rows")
    rank_size = basis_left.shape[2]
    for level_index in range(basis_left.shape[0], 0, -1):
        span_devices = devices >> level_index
        child_index = position // span_devices
        node_index = child_index // 2
        half_index = child_index % 2
        child_total = lax.dot_general(
            basis_right[level_index - 1],
            current,
            (((0,), (0,)), ((), ())),
            precision=highest,
            preferred_element_type=F32,
        )
        for bit_number in range(tree_depth - level_index):
            child_total = child_total + swapped(child_total, "rows", bit_number)
        sibling = swapped(child_total, "rows", tree_depth - level_index)
        stacked = jnp.where(
            half_index == 0,
            jnp.concatenate([child_total, sibling], axis=0),
            jnp.concatenate([sibling, child_total], axis=0),
        )
        core_block = lax.dynamic_index_in_dim(
            cores, 2 ** (level_index - 1) - 1 + node_index, 0, keepdims=False
        )
        core_rows = lax.dynamic_slice_in_dim(core_block, half_index * rank_size, rank_size, 0)
        coefficients = jnp.dot(core_rows, stacked, precision=highest, preferred_element_type=F32)
        current = current - jnp.dot(
            basis_left[level_index - 1], coefficients, precision=highest, preferred_element_type=F32
        )
    return current


def split(x):
    high = x.astype(BF16)
    return high, (x - high.astype(F32)).astype(BF16)


def weights(x):
    high, low = split(x)
    return jnp.concatenate([high, high, low], axis=1)


def values(x):
    high, low = split(x)
    return jnp.concatenate([high, low, high], axis=0)


def dot(a, b):
    return jnp.dot(a, b, preferred_element_type=F32)


def kernel(
    rhs_h, leaf_h, left_h, right_h, cores_h, out_h,
    rhs, leaf, left, right, core,
    leaf3, right3, left3, core3, x3, y3, coeff3,
    y, rest, own3, low2, low1, pair2, pair1, top, mix, upmix, c2s,
    in_sem, out_sem, send_sem, recv_sem,
):
    n, cols = rhs.shape
    rank = left.shape[2]
    chunks, _, _, wide = own3.shape
    half = x3.shape[1]
    me = lax.axis_index("rows")
    bit_y = lax.rem(me, 2)
    bit_z = lax.rem(me // 2, 2)
    bit_t = me // 4
    at_y = me + 1 - 2 * bit_y
    at_z = me + 2 - 4 * bit_z
    at_t = me + 4 - 8 * bit_t

    blocks = 4
    tall = n // blocks
    loads = []

    def load(src, dst):
        copy = pltpu.make_async_copy(src, dst, in_sem.at[len(loads)])
        copy.start()
        loads.append(copy)
        return copy

    load_right = load(right_h, right)
    load_left = load(left_h, left)
    load_rhs = load(rhs_h, rhs)
    load_leaf = [
        load(leaf_h.at[pl.ds(i * tall, tall), :], leaf.at[pl.ds(i * tall, tall), :])
        for i in range(blocks)
    ]
    load_core = [
        load(cores_h.at[3 + me // 2], core.at[2]),
        load(cores_h.at[1 + me // 4], core.at[1]),
        load(cores_h.at[0], core.at[0]),
    ]

    barrier = pltpu.get_barrier_semaphore()
    for other in (at_y, at_z, at_t):
        pl.semaphore_signal(
            barrier, inc=1, device_id={"rows": other}, device_id_type=pl.DeviceIdType.MESH
        )

    sends = []

    def send(ref, slot, other):
        k = len(sends)
        copy = pltpu.make_async_remote_copy(
            src_ref=ref.at[slot],
            dst_ref=ref.at[slot],
            send_sem=send_sem.at[k],
            recv_sem=recv_sem.at[k],
            device_id={"rows": other},
            device_id_type=pl.DeviceIdType.MESH,
        )
        copy.start()
        sends.append(copy)
        return copy

    load_right.wait()
    for i in range(3):
        right3[pl.ds(i * rank, rank), :] = weights(jnp.transpose(right[2 - i]))
    load_left.wait()
    mix[bit_y] = dot(right3[pl.ds(2 * rank, rank), :], values(left[1]))
    pl.semaphore_wait(barrier, 3)
    mix_y = send(mix, bit_y, at_y)
    mix3 = weights(dot(right3[pl.ds(rank, 2 * rank), :], values(left[2])))
    for i in range(3):
        left3[:, pl.ds(i * 3 * rank, 3 * rank)] = weights(left[2 - i])

    pieces = 2
    deep = n // pieces
    got = {}
    outs = []

    def leaf_piece(h, i):
        if i == 0:
            if h == 0:
                load_rhs.wait()
            x3[...] = values(rhs[:, pl.ds(h * half, half)])
        if h == 0:
            for j in range(i * blocks // pieces, (i + 1) * blocks // pieces):
                load_leaf[j].wait()
                leaf3[pl.ds(j * tall, tall), :] = weights(leaf[pl.ds(j * tall, tall), :])
        product = dot(leaf3[pl.ds(i * deep, deep), :], x3[...])
        high, low = split(product)
        y3[pl.ds(i * deep, deep), :] = high
        y3[pl.ds(n + i * deep, deep), :] = low
        y3[pl.ds(2 * n + i * deep, deep), :] = high
        for j in range(half // wide):
            y[h * half // wide + j, pl.ds(i * deep, deep), :] = product[:, j * wide:(j + 1) * wide]

    def project(h):
        partial = dot(right3[...], y3[...])
        for j in range(half // wide):
            c = h * half // wide + j
            own3[c, bit_y] = partial[:rank, j * wide:(j + 1) * wide]
            got["a", c] = send(own3.at[c], bit_y, at_y)
            rest[c] = partial[rank:, j * wide:(j + 1) * wide]

    def small():
        for copy in load_core:
            copy.wait()
        for i in range(3):
            core3[i] = weights(core[i])

    def middle():
        mix_y.wait_recv()
        upmix[bit_z] = mix[0] + mix[1]
        got["m"] = send(upmix, bit_z, at_z)

    def stack(ref, c):
        return values(jnp.concatenate([ref[c, 0], ref[c, 1]], axis=0))

    def third_level(c):
        got["a", c].wait_recv()
        coeff = values(dot(core3[2, pl.ds(bit_y * rank, rank), :], stack(own3, c)))
        reduced = rest[c] - dot(mix3, coeff)
        low2[c, bit_y] = reduced[:rank]
        got["b", c] = send(low2.at[c], bit_y, at_y)
        low1[c, bit_z] = reduced[rank:]
        got["c", c] = send(low1.at[c], bit_z, at_z)
        coeff3[c, pl.ds(0, 3 * rank), :] = coeff

    def pairs(c):
        got["b", c].wait_recv()
        pair2[c, bit_z] = low2[c, 0] + low2[c, 1]
        got["d", c] = send(pair2.at[c], bit_z, at_z)
        got["c", c].wait_recv()
        pair1[c, bit_y] = low1[c, 0] + low1[c, 1]
        got["e", c] = send(pair1.at[c], bit_y, at_y)

    def second_level(c):
        if "m3" not in got:
            got["m"].wait_recv()
            got["m3"] = weights(jnp.concatenate([upmix[0], upmix[1]], axis=1))
        got["d", c].wait_recv()
        coeff = dot(core3[1], stack(pair2, c))
        got["e", c].wait_recv()
        top[c, bit_t] = pair1[c, 0] + pair1[c, 1] - dot(got["m3"], values(coeff))
        got["f", c] = send(top.at[c], bit_t, at_t)
        c2s[0] = coeff[:rank]
        c2s[1] = coeff[rank:]
        coeff3[c, pl.ds(3 * rank, 3 * rank), :] = values(c2s[bit_z])
        y[c] = y[c] - dot(left3[:, pl.ds(0, 6 * rank)], coeff3[c])

    def first_level(c):
        got["f", c].wait_recv()
        coeff = values(dot(core3[0, pl.ds(bit_t * rank, rank), :], stack(top, c)))
        y[c] = y[c] - dot(left3[:, pl.ds(6 * rank, 3 * rank)], coeff)
        copy = pltpu.make_async_copy(y.at[c], out_h.at[:, pl.ds(c * wide, wide)], out_sem.at[c])
        copy.start()
        outs.append(copy)

    last = cols // half - 1
    per = half // wide
    for i in range(pieces):
        leaf_piece(0, i)
    project(0)
    small()
    for h in range(1, last + 1):
        before = range((h - 1) * per, h * per)
        leaf_piece(h, 0)
        if h == 1:
            middle()
        for c in before:
            third_level(c)
        for i in range(1, pieces):
            leaf_piece(h, i)
        project(h)
        for c in before:
            pairs(c)
    for c in range(last * per, chunks):
        third_level(c)
    ready = last * per
    for c in range(ready):
        second_level(c)
        if ready + c < chunks:
            pairs(ready + c)
    for c in range(ready + min(ready, per), chunks):
        pairs(c)
    for c in range(ready):
        first_level(c)
    for c in range(ready, chunks):
        second_level(c)
    for c in range(ready, chunks):
        first_level(c)

    for copy in sends:
        copy.wait_send()
    for copy in outs:
        copy.wait()


def on_device(rhs, leaf_inverse, basis_left, basis_right, cores):
    levels, n, rank = basis_left.shape
    cols = rhs.shape[1]
    if levels != 3 or lax.axis_size("rows") != 8 or cols % 512 or n % 1024 or rank % 128:
        return general(rhs, leaf_inverse, basis_left, basis_right, cores)
    wide = 128
    half = 256
    chunks = cols // wide
    hbm = pl.BlockSpec(memory_space=pltpu.HBM)
    dma = pltpu.SemaphoreType.DMA
    vmem = pltpu.VMEM
    swap = vmem((chunks, 2, rank, wide), F32)
    return pl.pallas_call(
        kernel,
        out_shape=pltpu.VMEM((n, cols), F32),
        in_specs=[hbm] * 5,
        out_specs=pl.BlockSpec(memory_space=pl.ANY),
        scratch_shapes=[
            vmem((n, cols), F32),
            vmem(leaf_inverse.shape, F32),
            vmem((3, n, rank), F32),
            vmem((3, n, rank), F32),
            vmem((3, 2 * rank, 2 * rank), F32),
            vmem((n, 3 * n), BF16),
            vmem((3 * rank, 3 * n), BF16),
            vmem((n, 9 * rank), BF16),
            vmem((3, 2 * rank, 6 * rank), BF16),
            vmem((3 * n, half), BF16),
            vmem((3 * n, half), BF16),
            vmem((chunks, 6 * rank, wide), BF16),
            vmem((chunks, n, wide), F32),
            vmem((chunks, 2 * rank, wide), F32),
            swap, swap, swap, swap, swap, swap,
            vmem((2, rank, rank), F32),
            vmem((2, rank, rank), F32),
            vmem((2, rank, wide), F32),
            dma((10,)),
            dma((chunks,)),
            dma((6 * chunks + 2,)),
            dma((6 * chunks + 2,)),
        ],
        compiler_params=pltpu.CompilerParams(
            collective_id=0, has_side_effects=True, vmem_limit_bytes=63000 * 1024
        ),
        name="tree",
    )(rhs, leaf_inverse, basis_left, basis_right, cores)


def solution(mesh):
    placed = (P("rows", "rhs"), P("rows", None), P(None, "rows", None), P(None, "rows", None), P())
    return jax.shard_map(
        on_device, mesh=mesh, in_specs=placed, out_specs=P("rows", "rhs"), check_vma=False
    )
```

```python
import jax
import jax.numpy as jnp
from jax import lax
from jax.experimental import pallas as pl
from jax.experimental.pallas import tpu as pltpu
from jax.sharding import PartitionSpec as P

F32 = jnp.float32
BF16 = jnp.bfloat16


def swapped(x, axis, apart):
    return lax.ppermute(x, axis, [(i, i ^ 1 << apart) for i in range(lax.axis_size(axis))])


def general(rhs, leaf_inverse, basis_left, basis_right, cores):
    highest = lax.Precision.HIGHEST
    current = jnp.dot(leaf_inverse, rhs, precision=highest, preferred_element_type=F32)
    devices = lax.axis_size("rows")
    tree_depth = devices.bit_length() - 1
    position = lax.axis_index("rows")
    rank_size = basis_left.shape[2]
    for level_index in range(basis_left.shape[0], 0, -1):
        span_devices = devices >> level_index
        child_index = position // span_devices
        node_index = child_index // 2
        half_index = child_index % 2
        child_total = lax.dot_general(
            basis_right[level_index - 1],
            current,
            (((0,), (0,)), ((), ())),
            precision=highest,
            preferred_element_type=F32,
        )
        for bit_number in range(tree_depth - level_index):
            child_total = child_total + swapped(child_total, "rows", bit_number)
        sibling = swapped(child_total, "rows", tree_depth - level_index)
        stacked = jnp.where(
            half_index == 0,
            jnp.concatenate([child_total, sibling], axis=0),
            jnp.concatenate([sibling, child_total], axis=0),
        )
        core_block = lax.dynamic_index_in_dim(
            cores, 2 ** (level_index - 1) - 1 + node_index, 0, keepdims=False
        )
        core_rows = lax.dynamic_slice_in_dim(core_block, half_index * rank_size, rank_size, 0)
        coefficients = jnp.dot(core_rows, stacked, precision=highest, preferred_element_type=F32)
        current = current - jnp.dot(
            basis_left[level_index - 1], coefficients, precision=highest, preferred_element_type=F32
        )
    return current


def split(x):
    high = x.astype(BF16)
    return high, (x - high.astype(F32)).astype(BF16)


def weights(x):
    high, low = split(x)
    return jnp.concatenate([high, high, low], axis=1)


def values(x):
    high, low = split(x)
    return jnp.concatenate([high, low, high], axis=0)


def dot(a, b):
    return jnp.dot(a, b, preferred_element_type=F32)


def kernel(
    rhs_h, leaf_h, left_h, right_h, cores_h, out_h,
    rhs, leaf, left, right, core,
    leaf3, right3, left3, core3, x3, y3, coeff3,
    y, rest, own3, low2, low1, pair2, pair1, top, mix, upmix, c2s,
    in_sem, out_sem, send_sem, recv_sem,
):
    n, cols = rhs.shape
    rank = left.shape[2]
    chunks, _, _, wide = own3.shape
    half = x3.shape[1]
    me = lax.axis_index("rows")
    bit_y = lax.rem(me, 2)
    bit_z = lax.rem(me // 2, 2)
    bit_t = me // 4
    at_y = me + 1 - 2 * bit_y
    at_z = me + 2 - 4 * bit_z
    at_t = me + 4 - 8 * bit_t

    blocks = 4
    tall = n // blocks
    loads = []

    def load(src, dst):
        copy = pltpu.make_async_copy(src, dst, in_sem.at[len(loads)])
        copy.start()
        loads.append(copy)
        return copy

    load_rhs = load(rhs_h, rhs)
    load_leaf = [
        load(leaf_h.at[pl.ds(i * tall, tall), :], leaf.at[pl.ds(i * tall, tall), :])
        for i in range(blocks)
    ]
    load_right = load(right_h, right)
    load_left = load(left_h, left)
    load_core = [
        load(cores_h.at[3 + me // 2], core.at[2]),
        load(cores_h.at[1 + me // 4], core.at[1]),
        load(cores_h.at[0], core.at[0]),
    ]

    barrier = pltpu.get_barrier_semaphore()
    for other in (at_y, at_z, at_t):
        pl.semaphore_signal(
            barrier, inc=1, device_id={"rows": other}, device_id_type=pl.DeviceIdType.MESH
        )

    sends = []

    def send(ref, slot, other):
        k = len(sends)
        copy = pltpu.make_async_remote_copy(
            src_ref=ref.at[slot],
            dst_ref=ref.at[slot],
            send_sem=send_sem.at[k],
            recv_sem=recv_sem.at[k],
            device_id={"rows": other},
            device_id_type=pl.DeviceIdType.MESH,
        )
        copy.start()
        sends.append(copy)
        return copy

    pieces = 2
    deep = n // pieces
    got = {}
    outs = []

    def leaf_piece(h, i):
        if i == 0:
            if h == 0:
                load_rhs.wait()
            x3[...] = values(rhs[:, pl.ds(h * half, half)])
        if h == 0:
            for j in range(i * blocks // pieces, (i + 1) * blocks // pieces):
                load_leaf[j].wait()
                leaf3[pl.ds(j * tall, tall), :] = weights(leaf[pl.ds(j * tall, tall), :])
        product = dot(leaf3[pl.ds(i * deep, deep), :], x3[...])
        high, low = split(product)
        y3[pl.ds(i * deep, deep), :] = high
        y3[pl.ds(n + i * deep, deep), :] = low
        y3[pl.ds(2 * n + i * deep, deep), :] = high
        for j in range(half // wide):
            y[h * half // wide + j, pl.ds(i * deep, deep), :] = product[:, j * wide:(j + 1) * wide]

    def project(h):
        if h == 0:
            load_right.wait()
            for i in range(3):
                right3[pl.ds(i * rank, rank), :] = weights(jnp.transpose(right[2 - i]))
            pl.semaphore_wait(barrier, 3)
        partial = dot(right3[...], y3[...])
        for j in range(half // wide):
            c = h * half // wide + j
            own3[c, bit_y] = partial[:rank, j * wide:(j + 1) * wide]
            got["a", c] = send(own3.at[c], bit_y, at_y)
            rest[c] = partial[rank:, j * wide:(j + 1) * wide]

    def small():
        load_left.wait()
        got["mix3"] = weights(dot(right3[pl.ds(rank, 2 * rank), :], values(left[2])))
        mix[bit_y] = dot(right3[pl.ds(2 * rank, rank), :], values(left[1]))
        got["n"] = send(mix, bit_y, at_y)
        for copy in load_core:
            copy.wait()
        core3[2] = weights(core[2])

    def prepare():
        for i in range(2):
            core3[i] = weights(core[i])
        for i in range(3):
            left3[:, pl.ds(i * 3 * rank, 3 * rank)] = weights(left[2 - i])

    def middle():
        got["n"].wait_recv()
        upmix[bit_z] = mix[0] + mix[1]
        got["m"] = send(upmix, bit_z, at_z)

    def stack(ref, c):
        return values(jnp.concatenate([ref[c, 0], ref[c, 1]], axis=0))

    def third_level(c):
        got["a", c].wait_recv()
        coeff = values(dot(core3[2, pl.ds(bit_y * rank, rank), :], stack(own3, c)))
        reduced = rest[c] - dot(got["mix3"], coeff)
        low2[c, bit_y] = reduced[:rank]
        got["b", c] = send(low2.at[c], bit_y, at_y)
        low1[c, bit_z] = reduced[rank:]
        got["c", c] = send(low1.at[c], bit_z, at_z)
        coeff3[c, pl.ds(0, 3 * rank), :] = coeff

    def pairs(c):
        got["b", c].wait_recv()
        pair2[c, bit_z] = low2[c, 0] + low2[c, 1]
        got["d", c] = send(pair2.at[c], bit_z, at_z)
        got["c", c].wait_recv()
        pair1[c, bit_y] = low1[c, 0] + low1[c, 1]
        got["e", c] = send(pair1.at[c], bit_y, at_y)

    def second_level(c):
        if "m3" not in got:
            got["m"].wait_recv()
            got["m3"] = weights(jnp.concatenate([upmix[0], upmix[1]], axis=1))
        got["d", c].wait_recv()
        coeff = dot(core3[1], stack(pair2, c))
        got["e", c].wait_recv()
        top[c, bit_t] = pair1[c, 0] + pair1[c, 1] - dot(got["m3"], values(coeff))
        got["f", c] = send(top.at[c], bit_t, at_t)
        c2s[0] = coeff[:rank]
        c2s[1] = coeff[rank:]
        coeff3[c, pl.ds(3 * rank, 3 * rank), :] = values(c2s[bit_z])

    def update(c):
        y[c] = y[c] - dot(left3[:, pl.ds(0, 6 * rank)], coeff3[c])

    def first_level(c):
        got["f", c].wait_recv()
        coeff = values(dot(core3[0, pl.ds(bit_t * rank, rank), :], stack(top, c)))
        y[c] = y[c] - dot(left3[:, pl.ds(6 * rank, 3 * rank)], coeff)
        copy = pltpu.make_async_copy(y.at[c], out_h.at[:, pl.ds(c * wide, wide)], out_sem.at[c])
        copy.start()
        outs.append(copy)

    last = cols // half - 1
    per = half // wide
    for i in range(pieces):
        leaf_piece(0, i)
    project(0)
    small()
    for h in range(1, last + 1):
        before = range((h - 1) * per, h * per)
        leaf_piece(h, 0)
        for c in before:
            third_level(c)
        for i in range(1, pieces):
            leaf_piece(h, i)
        project(h)
        if h == 1:
            middle()
        for c in before:
            pairs(c)
        if h == 1:
            prepare()
    for c in range(last * per, chunks):
        third_level(c)
    ready = last * per
    for c in range(ready):
        second_level(c)
        if ready + c < chunks:
            pairs(ready + c)
    for c in range(ready + min(ready, per), chunks):
        pairs(c)
    for c in range(ready):
        update(c)
    for c in range(ready, chunks):
        second_level(c)
    for c in range(ready, chunks):
        update(c)
    for c in range(chunks):
        first_level(c)

    for copy in sends:
        copy.wait_send()
    for copy in outs:
        copy.wait()


def on_device(rhs, leaf_inverse, basis_left, basis_right, cores):
    levels, n, rank = basis_left.shape
    cols = rhs.shape[1]
    if levels != 3 or lax.axis_size("rows") != 8 or cols % 512 or n % 1024 or rank % 128:
        return general(rhs, leaf_inverse, basis_left, basis_right, cores)
    wide = 128
    half = 256
    chunks = cols // wide
    hbm = pl.BlockSpec(memory_space=pltpu.HBM)
    dma = pltpu.SemaphoreType.DMA
    vmem = pltpu.VMEM
    swap = vmem((chunks, 2, rank, wide), F32)
    return pl.pallas_call(
        kernel,
        out_shape=pltpu.VMEM((n, cols), F32),
        in_specs=[hbm] * 5,
        out_specs=pl.BlockSpec(memory_space=pl.ANY),
        scratch_shapes=[
            vmem((n, cols), F32),
            vmem(leaf_inverse.shape, F32),
            vmem((3, n, rank), F32),
            vmem((3, n, rank), F32),
            vmem((3, 2 * rank, 2 * rank), F32),
            vmem((n, 3 * n), BF16),
            vmem((3 * rank, 3 * n), BF16),
            vmem((n, 9 * rank), BF16),
            vmem((3, 2 * rank, 6 * rank), BF16),
            vmem((3 * n, half), BF16),
            vmem((3 * n, half), BF16),
            vmem((chunks, 6 * rank, wide), BF16),
            vmem((chunks, n, wide), F32),
            vmem((chunks, 2 * rank, wide), F32),
            swap, swap, swap, swap, swap, swap,
            vmem((2, rank, rank), F32),
            vmem((2, rank, rank), F32),
            vmem((2, rank, wide), F32),
            dma((10,)),
            dma((chunks,)),
            dma((6 * chunks + 2,)),
            dma((6 * chunks + 2,)),
        ],
        compiler_params=pltpu.CompilerParams(
            collective_id=0, has_side_effects=True, vmem_limit_bytes=63000 * 1024
        ),
        name="tree",
    )(rhs, leaf_inverse, basis_left, basis_right, cores)


def solution(mesh):
    placed = (P("rows", "rhs"), P("rows", None), P(None, "rows", None), P(None, "rows", None), P())
    return jax.shard_map(
        on_device, mesh=mesh, in_specs=placed, out_specs=P("rows", "rhs"), check_vma=False
    )
```
